256 devices in a mesh: frame: 64 (over y, z, x_lo), band: 4 (over x_hi, core).
Axes of the slice: x: 4 (x_hi: 2, x_lo: 2; x = x_hi * 2 + x_lo), y: 4, z: 8, core: 2. Of those that a mesh axis runs over, the one named last changes fastest.
Arguments:
- latents: bfloat16 [64, 64, 32, 640], P('frame', 'band'), may hold values from -90 to 90, as said below
- conv_weight: bfloat16 [3, 3, 640, 640], replicated, may hold values from -0.078125 to 0.078125
- conv_bias: bfloat16 [640], replicated, may hold values from -3 to 3
- w_query: bfloat16 [640, 640], replicated, may hold values from -0.25 to 0.25
- w_keyval: bfloat16 [640, 1280], replicated, may hold values from -0.25 to 0.25
- w_out: bfloat16 [640, 640], replicated, may hold values from -0.25 to 0.25
Outputs:
- result: bfloat16 [64, 64, 32, 640], P('frame', 'band')
The draws below stay inside these ranges and needn't reach their ends.
Inputs may be any that keep to these rules, and one draw needn't show every extreme that they name: `latents`: latent features; some frames may be far larger in magnitude than others.
All inputs are finite; a program needn't handle non-finite values.
Results may differ from the reference program's by a relative error of at most 0.023.
Values may be sent and summed in bfloat16 or wider, within the bound.
A program may use at most 128 MiB of HBM per device.

```python
import jax
import jax.numpy as jnp
from jax import lax

CHANNELS = 640
HEAD_DIM = 64
WIDTH = 32
HEADS = 10
FRAMES = 64
HEIGHT = 64


def draw_latents(key, part):
    values = jax.random.normal(jax.random.fold_in(key, 11), (FRAMES, HEIGHT, WIDTH, CHANNELS), jnp.float32)
    values = jnp.clip(values, -5.0, 5.0)
    return values.astype(jnp.bfloat16)


def bell_draw(own_key, dims, width, limit, held_as=jnp.bfloat16):
    entries = width * jax.random.normal(own_key, dims, jnp.float32)
    return jnp.clip(entries, min=-limit, max=limit).astype(held_as)


def setup_inputs(seed: int = 0) -> dict:
    splits = jax.random.split(jax.random.key(seed), 7)
    return {
        "latents": draw_latents(jax.random.fold_in(splits[6], 71), 0),
        "conv_weight": bell_draw(splits[1], (3, 3, CHANNELS, CHANNELS), (9 * CHANNELS) ** -0.5, 0.078125),
        "conv_bias": bell_draw(splits[2], (CHANNELS,), 0.5, 3.0),
        "w_query": bell_draw(splits[3], (CHANNELS, CHANNELS), CHANNELS ** -0.5, 0.25),
        "w_keyval": bell_draw(splits[4], (CHANNELS, 2 * CHANNELS), CHANNELS ** -0.5, 0.25),
        "w_out": bell_draw(splits[5], (CHANNELS, CHANNELS), CHANNELS ** -0.5, 0.25),
    }


def conv_frame(frame, conv_weight, conv_bias):
    activated = jax.nn.silu(frame.astype(jnp.float32)).astype(jnp.bfloat16)
    padded = jnp.pad(activated, ((1, 1), (1, 1), (0, 0)))
    row_count, col_count, channels = frame.shape
    tokens = row_count * col_count
    summed = jnp.zeros((tokens, channels), jnp.float32)
    for row_shift in range(3):
        for col_shift in range(3):
            window = padded[row_shift:row_shift + row_count, col_shift:col_shift + col_count].reshape(tokens, channels)
            summed = summed + jnp.dot(window, conv_weight[row_shift, col_shift], preferred_element_type=jnp.float32)
    hidden = frame.reshape(tokens, channels).astype(jnp.float32) + summed + conv_bias.astype(jnp.float32)
    return hidden.astype(jnp.bfloat16)


def attend_all(queries, keys, values):
    query_count = queries.shape[0]
    key_count = keys.shape[0]
    query_heads = queries.reshape(query_count, HEADS, HEAD_DIM).astype(jnp.float32)
    key_heads = keys.reshape(key_count, HEADS, HEAD_DIM).astype(jnp.float32)
    value_heads = values.reshape(key_count, HEADS, HEAD_DIM).astype(jnp.float32)
    scores = jnp.einsum("qhd,khd->hqk", query_heads, key_heads) * (HEAD_DIM ** -0.5)
    row_best = jnp.max(scores, axis=2, keepdims=True)
    probability = jnp.exp(scores - row_best)
    total = jnp.sum(probability, axis=2)
    rounded = probability.astype(jnp.bfloat16).astype(jnp.float32)
    mixed = jnp.einsum("hqk,khd->qhd", rounded, value_heads)
    mixed = mixed / jnp.transpose(total)[:, :, None]
    return mixed.reshape(query_count, CHANNELS).astype(jnp.bfloat16)


def reference(latents, conv_weight, conv_bias, w_query, w_keyval, w_out):
    hidden = lax.map(lambda frame: conv_frame(frame, conv_weight, conv_bias), latents)
    keyval = jnp.dot(hidden[0], w_keyval, preferred_element_type=jnp.float32).astype(jnp.bfloat16)
    keys = keyval[:, :CHANNELS]
    values = keyval[:, CHANNELS:]

    def one_frame(frame_tokens):
        queries = jnp.dot(frame_tokens, w_query, preferred_element_type=jnp.float32).astype(jnp.bfloat16)
        mixed = attend_all(queries, keys, values)
        output = frame_tokens.astype(jnp.float32) + jnp.dot(mixed, w_out, preferred_element_type=jnp.float32)
        return output.astype(jnp.bfloat16)

    result = lax.map(one_frame, hidden)
    return result.reshape(FRAMES, HEIGHT, WIDTH, CHANNELS)
```

```python
import jax
import jax.numpy as jnp
from jax import lax
from jax.experimental import pallas as pl
from jax.experimental.pallas import tpu as pltpu
from jax.sharding import PartitionSpec as P

BF = jnp.bfloat16
F32 = jnp.float32
MESH = pl.DeviceIdType.MESH
ROWS, COLS, C = 16, 32, 640
TOK = ROWS * COLS
KEYS = 4 * TOK
CH = 32
NCH = TOK // CH
LAG = 8
SCALE = 0.125 * 1.4426950408889634

TABLE = (
    (
        (1436916138, -2057218667, -1442141558, -1470609788, 0, 0, 5376, 268435456),
        (1788127785, 627464597, 0, 0, 0, 0, 1434801189, 1436913753),
        (-1434081239, 4456464, -1610046968, 1146093568, 18874400, 5242880, 562473, 2048),
        (1074833577, 1076363344, 336392, 167772176, 512, 671088656, 37513, -1539309568),
        (-2139029462, 8454224, 0, 360472, 0, -2147450880, 4129, 8),
        (1409394690, 67702792, 537395200, 1611202560, 1024, 0, 529736, 4261896),
        (524288, 262145, 0, 0, 0, 0, 0, 0),
        (0, 1073741825, 67117058, 134217728, 67108864, 0, 67108865, 0),
    ),
    (
        (0, 0, 2097184, 131104, -1705399670, 1686720645, 1435861144, 1113957700),
        (0, 0, -1469437406, -1717937510, -1441158566, -1722216432, 0, 0),
        (2097664, 1342252032, 178323586, 268780544, 1753918089, 1074004992, -1974337408, 1342472192),
        (88342528, 65536, 1073741986, -2142632960, 357607593, -2112815104, 89196576, 2629632),
        (0, 0, 5243232, 134217729, 5243010, 9437249, -2146893816, 9764864),
        (0, 0, 1074855936, 1086465, 1343856642, 1074860032, 65536, 1074302976),
        (0, 0, 131074, 2097152, 65544, 65540, 1048576, 16),
        (0, 0, 0, 0, 0, 268435457, 1073741824, 268435456),
    ),
)

STEPS = ((1, 0, 0), (-1, 0, 0), (0, 1, 0), (0, -1, 0), (0, 0, 1), (0, 0, -1), (0, 0, 2), (0, 0, -2))


def lookup(words, word, bit):
    value = jnp.int32(words[0])
    for k in range(1, 8):
        value = jnp.where(word == k, jnp.int32(words[k]), value)
    return lax.shift_right_logical(value, bit) & 1


def silu(v):
    v = v.astype(F32)
    return v * jax.nn.sigmoid(v)


def place(pad, act, row0):
    n = act.shape[0]
    col = lax.broadcasted_iota(jnp.int32, (n, 1), 0) % COLS
    pad[1, row0 : row0 + n] = act.astype(BF)
    pad[0, row0 : row0 + n] = jnp.where(col == 0, 0.0, pltpu.roll(act, 1, 0)).astype(BF)
    pad[2, row0 : row0 + n] = jnp.where(col == COLS - 1, 0.0, pltpu.roll(act, n - 1, 0)).astype(BF)


def spread_kernel(
    x_ref, w_hbm, b_ref, wq_ref, hid_ref, q_ref, h0_ref,
    wbuf, pad, halo, acc, wsem, hsend, hrecv, recv, send,
):
    f = lax.axis_index("frame")
    b = lax.axis_index("band")
    core = b % 2
    x = (b // 2) * 2 + f % 2
    y = f // 16
    z = (f // 2) % 8

    def chip(step):
        nx, ny, nz = (x + step[0] + 4) % 4, (y + step[1] + 4) % 4, (z + step[2] + 8) % 8
        return (ny * 16 + nz * 2 + nx % 2, (nx // 2) * 2 + core)

    targets = [chip(step) for step in STEPS]
    partner = (f, b + 1 - 2 * core)

    weights = [pltpu.make_async_copy(w_hbm.at[i], wbuf.at[i], wsem.at[i]) for i in range(3)]
    for i in (1, 0, 2):
        weights[i].start()

    barrier = pltpu.get_barrier_semaphore()
    for target in targets + [partner]:
        pl.semaphore_signal(barrier, inc=1, device_id=target, device_id_type=MESH)
    middle = (b == 1) | (b == 2)

    @pl.when(middle)
    def _():
        pl.semaphore_signal(barrier, inc=1, device_id=(f, 3 - b), device_id_type=MESH)

    pl.semaphore_wait(barrier, jnp.where(middle, 10, 9))

    def halo_copy(rows, slot, target):
        return pltpu.make_async_remote_copy(
            src_ref=x_ref.at[pl.ds(rows, COLS)], dst_ref=halo.at[slot],
            send_sem=hsend.at[slot], recv_sem=hrecv.at[slot],
            device_id=target, device_id_type=MESH,
        )

    up = halo_copy(0, 1, (f, jnp.maximum(b - 1, 0)))
    down = halo_copy(TOK - COLS, 0, (f, jnp.minimum(b + 1, 3)))

    @pl.when(b > 0)
    def _():
        up.start()

    @pl.when(b < 3)
    def _():
        down.start()

    place(pad, silu(x_ref[...]), COLS)
    acc[...] = x_ref[...].astype(F32) + b_ref[...].astype(F32)

    def tap(i):
        weights[i].wait()
        window = jnp.concatenate([pad[c, i * COLS : i * COLS + TOK] for c in range(3)], axis=1)
        acc[...] += jnp.dot(window, wbuf[i], preferred_element_type=F32)

    tap(1)

    @pl.when(b > 0)
    def _():
        up.wait_send()
        down.wait_recv()
        place(pad, silu(halo[0]), 0)

    @pl.when(b == 0)
    def _():
        pad[:, 0:COLS] = jnp.zeros((3, COLS, C), BF)

    @pl.when(b < 3)
    def _():
        down.wait_send()
        up.wait_recv()
        place(pad, silu(halo[1]), TOK + COLS)

    @pl.when(b == 3)
    def _():
        pad[:, TOK + COLS :] = jnp.zeros((3, COLS, C), BF)

    tap(0)
    tap(2)
    hidden = acc[...].astype(BF)
    hid_ref[...] = hidden

    @pl.when(f == 0)
    def _():
        h0_ref[pl.ds(pl.multiple_of(b * TOK, TOK), TOK), :] = hidden

    q_ref[...] = (jnp.dot(hidden, wq_ref[...], preferred_element_type=F32) * SCALE).astype(BF)

    index = ((x * 4 + y) * 8 + z) * 2 + core
    flags = [[lookup(TABLE[g][a], index // 32, index % 32) for a in range(8)] for g in range(2)]
    lags = [jnp.where(x == 2, LAG, 0), jnp.where(x == 0, LAG, 0)]

    def piece(band, k, g, arc, target):
        rows = h0_ref.at[pl.ds(pl.multiple_of(band * TOK + k * CH, CH), CH)]
        return pltpu.make_async_remote_copy(
            src_ref=rows, dst_ref=rows, send_sem=send.at[g, k, arc], recv_sem=recv.at[band, k],
            device_id=target, device_id_type=MESH,
        )

    def slot(s, _):
        for g in range(2):
            band = core + 2 * g
            k = s - lags[g]

            @pl.when((k >= 0) & (k < NCH))
            def _():
                @pl.when((f != 0) | (b != band))
                def _():
                    piece(band, k, g, 8, partner).wait_recv()

                for a in range(8):
                    @pl.when(flags[g][a] == 1)
                    def _():
                        piece(band, k, g, a, targets[a]).start()

                piece(band, k, g, 8, partner).start()

        return 0

    lax.fori_loop(0, NCH + LAG, slot, 0)

    def finish(k, _):
        for g in range(2):
            band = core + 2 * g
            for a in range(8):
                @pl.when(flags[g][a] == 1)
                def _():
                    piece(band, k, g, a, targets[a]).wait_send()

            piece(band, k, g, 8, partner).wait_send()
            piece(1 - core + 2 * g, k, g, 8, partner).wait_recv()
        return 0

    lax.fori_loop(0, NCH, finish, 0)


def attend_kernel(h_ref, q_ref, h0_ref, wkv_ref, wout_ref, o_ref, keys, values, mix):
    lane = lax.broadcasted_iota(jnp.int32, (1, 128), 1)
    values[:, 128:] = jnp.ones((KEYS, 128), BF)
    block = 128

    @pl.loop(0, 5)
    def _(j):
        c = pl.multiple_of(j * 128, 128)
        w = jnp.concatenate([wkv_ref[:, pl.ds(c, 128)], wkv_ref[:, pl.ds(pl.multiple_of(C + c, 128), 128)]], axis=1)
        kv = jnp.dot(h0_ref[...], w, preferred_element_type=F32).astype(BF)
        keys[...] = kv[:, :128]
        values[:, :128] = kv[:, 128:]
        for half in range(2):
            keep = (lane < 64) if half == 0 else (lane >= 64)
            for r in range(TOK // block):
                rows = slice(r * block, (r + 1) * block)
                head = jnp.where(keep, q_ref[rows, pl.ds(c, 128)], jnp.zeros((), BF))
                scores = lax.dot_general(head, keys[...], (((1,), (1,)), ((), ())), preferred_element_type=F32)
                best = jnp.max(scores, axis=1, keepdims=True)
                prob = jnp.exp2(scores - best).astype(BF)
                out = jnp.dot(prob, values[...], preferred_element_type=F32)
                out = (out[:, :128] / out[:, 128:]).astype(BF)
                if half == 1:
                    out = jnp.where(keep, out, mix[rows, pl.ds(c, 128)])
                mix[rows, pl.ds(c, 128)] = out

    o_ref[...] = (
        h_ref[...].astype(F32) + jnp.dot(mix[...], wout_ref[...], preferred_element_type=F32)
    ).astype(BF)


def per_device(latents, conv_weight, conv_bias, w_query, w_keyval, w_out):
    vmem = pl.BlockSpec(memory_space=pltpu.VMEM)
    tokens = jax.ShapeDtypeStruct((TOK, C), BF)
    hidden, queries, first = pl.pallas_call(
        spread_kernel,
        out_shape=[tokens, tokens, jax.ShapeDtypeStruct((KEYS, C), BF)],
        in_specs=[vmem, pl.BlockSpec(memory_space=pl.ANY), vmem, vmem],
        out_specs=[vmem, vmem, vmem],
        scratch_shapes=[
            pltpu.VMEM((3, 3 * C, C), BF),
            pltpu.VMEM((3, TOK + 2 * COLS, C), BF),
            pltpu.VMEM((2, COLS, C), BF),
            pltpu.VMEM((TOK, C), F32),
            pltpu.SemaphoreType.DMA((3,)),
            pltpu.SemaphoreType.DMA((2,)),
            pltpu.SemaphoreType.DMA((2,)),
            pltpu.SemaphoreType.DMA((4, NCH)),
            pltpu.SemaphoreType.DMA((2, NCH, 9)),
        ],
        compiler_params=pltpu.CompilerParams(collective_id=0, has_side_effects=True),
        name="spread",
    )(latents.reshape(TOK, C), conv_weight.reshape(3, 3 * C, C), conv_bias.reshape(1, C), w_query)
    result = pl.pallas_call(
        attend_kernel,
        out_shape=tokens,
        in_specs=[vmem] * 5,
        out_specs=vmem,
        scratch_shapes=[
            pltpu.VMEM((KEYS, 128), BF),
            pltpu.VMEM((KEYS, 256), BF),
            pltpu.VMEM((TOK, C), BF),
        ],
        name="attend",
    )(hidden, queries, first, w_keyval, w_out)
    return result.reshape(latents.shape)


def solution(mesh):
    return jax.shard_map(
        per_device,
        mesh=mesh,
        in_specs=(P("frame", "band", None, None), P(), P(), P(), P(), P()),
        out_specs=P("frame", "band", None, None),
        check_vma=False,
    )
```

```python
import jax
import jax.numpy as jnp
from jax import lax
from jax.experimental import pallas as pl
from jax.experimental.pallas import tpu as pltpu
from jax.sharding import PartitionSpec as P

BF = jnp.bfloat16
F32 = jnp.float32
MESH = pl.DeviceIdType.MESH
ROWS, COLS, C = 16, 32, 640
TOK = ROWS * COLS
KEYS = 4 * TOK
NCH = 8
PART = TOK // 2
CH = PART // NCH
SCALE = 0.125 * 1.4426950408889634

ARCS = (
    (
        (157049088, -1860284160, 0, 4),
        (92823553, 0, 2, 1860249119),
        (-2011160575, -1946156796, -2147483648, -2147454715),
        (-1929092543, 160064, 24576, 67133456),
        (201408768, 402718720, 16384, 83969292),
        (83914784, 88150272, 0, -2130706428),
        (16777216, 16777216, 0, 134217729),
        (4260096, 16384, 8192, 16384),
    ),
    (
        (1923194619, 1858111199, 0, 0),
        (-1337942274, 0, 0, -1878894304),
        (50406, 16896, 6176, 265216),
        (570425518, 402653325, 603979776, -2113929142),
        (8947727, 135170, 0, -2146955264),
        (-2113929023, 33280, 33685504, 164354),
        (131584, 0, 0, 0),
        (1073741824, 0, 0, 8388608),
    ),
    (
        (0, 0, -1188287234, -1281251928),
        (1073741824, 1280065620, -1226251028, 0),
        (24, 1050, 18398, 32960),
        (268435456, 33554432, -2013265684, 268435460),
        (128, -2071953280, -2147450868, 10520704),
        (263172, -2147483644, 69222597, 67372032),
        (0, 262148, 67108865, 0),
        (0, 0, 8388608, 0),
    ),
    (
        (0, 8224, 1112625921, 1279541328),
        (0, 867286947, 1090914817, 128),
        (2560, 1074043105, 1409318913, 100663840),
        (3072, 1627393058, 1392511489, 536871073),
        (1073741824, 1073741825, 1393821952, 33948160),
        (0, 268435489, 268470528, 268505585),
        (0, 1280, 66048, 0),
        (0, 1073741952, 1090519040, 1073741824),
    ),
)
LAGS = (
    ((0, 0, 0, 0), (1644203262, 1644171005, -536905953, 536903906), (1644201084, 301992000, 1879076992, 1342210146), (2178, 1610614461, -63713, 128), (0, 2, 35040, 0)),
    ((0, 0, 0, 0), (16843008, 73984, -16843011, 83960065), (208953344, 2088522796, 1567950110, 1549030428), (16843008, 74000, -16843011, 83960065), (0, 0, 16843008, 0)),
    ((0, 0, 0, 0), (-50529028, 50529027, 50529024, 1128465155), (289502477, 1648517666, 1112670720, 1107456514), (-318969632, 16843009, 16843008, 1094779137), (50529027, 0, 0, 0)),
    ((0, 0, 0, 0), (2013265907, -1946140596, -1474288388, 134219790), (1946440736, -2013265840, -1944051594, 204239900), (134212563, 67125260, 1164, 2062), (-2013265908, 0, 0, 0)),
)
MAXLAG = 20


STEPS = ((1, 0, 0), (-1, 0, 0), (0, 1, 0), (0, -1, 0), (0, 0, 1), (0, 0, -1), (0, 0, 2), (0, 0, -2))


def lookup(words, word, bit):
    value = jnp.int32(words[0])
    for k in range(1, 4):
        value = jnp.where(word == k, jnp.int32(words[k]), value)
    return lax.shift_right_logical(value, bit) & 1


def silu(v):
    v = v.astype(F32)
    return v * jax.nn.sigmoid(v)


def place(pad, act, row0):
    n = act.shape[0]
    col = lax.broadcasted_iota(jnp.int32, (n, 1), 0) % COLS
    pad[1, row0 : row0 + n] = act.astype(BF)
    pad[0, row0 : row0 + n] = jnp.where(col == 0, 0.0, pltpu.roll(act, 1, 0)).astype(BF)
    pad[2, row0 : row0 + n] = jnp.where(col == COLS - 1, 0.0, pltpu.roll(act, n - 1, 0)).astype(BF)


def spread_kernel(
    x_ref, w_hbm, b_ref, wq_ref, hid_ref, q_ref, h0_ref,
    wbuf, pad, halo, acc, wsem, hsend, hrecv, recv, send,
):
    f = lax.axis_index("frame")
    b = lax.axis_index("band")
    core = b % 2
    x = (b // 2) * 2 + f % 2
    y = f // 16
    z = (f // 2) % 8

    def chip(step):
        nx, ny, nz = (x + step[0] + 4) % 4, (y + step[1] + 4) % 4, (z + step[2] + 8) % 8
        return (ny * 16 + nz * 2 + nx % 2, (nx // 2) * 2 + core)

    targets = [chip(step) for step in STEPS]
    partner = (f, b + 1 - 2 * core)

    weights = [pltpu.make_async_copy(w_hbm.at[i], wbuf.at[i], wsem.at[i]) for i in range(3)]
    for i in (1, 0, 2):
        weights[i].start()

    barrier = pltpu.get_barrier_semaphore()
    for target in targets + [partner]:
        pl.semaphore_signal(barrier, inc=1, device_id=target, device_id_type=MESH)
    middle = (b == 1) | (b == 2)

    @pl.when(middle)
    def _():
        pl.semaphore_signal(barrier, inc=1, device_id=(f, 3 - b), device_id_type=MESH)

    pl.semaphore_wait(barrier, jnp.where(middle, 10, 9))

    def halo_copy(rows, slot, target):
        return pltpu.make_async_remote_copy(
            src_ref=x_ref.at[pl.ds(rows, COLS)], dst_ref=halo.at[slot],
            send_sem=hsend.at[slot], recv_sem=hrecv.at[slot],
            device_id=target, device_id_type=MESH,
        )

    up = halo_copy(0, 1, (f, jnp.maximum(b - 1, 0)))
    down = halo_copy(TOK - COLS, 0, (f, jnp.minimum(b + 1, 3)))

    @pl.when(b > 0)
    def _():
        up.start()

    @pl.when(b < 3)
    def _():
        down.start()

    place(pad, silu(x_ref[...]), COLS)
    acc[...] = x_ref[...].astype(F32) + b_ref[...].astype(F32)

    def tap(i):
        weights[i].wait()
        window = jnp.concatenate([pad[c, i * COLS : i * COLS + TOK] for c in range(3)], axis=1)
        acc[...] += jnp.dot(window, wbuf[i], preferred_element_type=F32)

    tap(1)

    @pl.when(b > 0)
    def _():
        up.wait_send()
        down.wait_recv()
        place(pad, silu(halo[0]), 0)

    @pl.when(b == 0)
    def _():
        pad[:, 0:COLS] = jnp.zeros((3, COLS, C), BF)

    @pl.when(b < 3)
    def _():
        down.wait_send()
        up.wait_recv()
        place(pad, silu(halo[1]), TOK + COLS)

    @pl.when(b == 3)
    def _():
        pad[:, TOK + COLS :] = jnp.zeros((3, COLS, C), BF)

    tap(0)
    tap(2)
    hidden = acc[...].astype(BF)
    hid_ref[...] = hidden

    @pl.when(f == 0)
    def _():
        h0_ref[pl.ds(pl.multiple_of(b * TOK, TOK), TOK), :] = hidden

    q_ref[...] = (jnp.dot(hidden, wq_ref[...], preferred_element_type=F32) * SCALE).astype(BF)

    index = (x * 4 + y) * 8 + z
    word, bit = index // 32, index % 32
    flags = [[lookup(words, word, bit) if any(words) else None for words in ARCS[g]] for g in range(4)]
    lags = [sum(lookup(words, word, bit) * 2**i for i, words in enumerate(LAGS[g])) for g in range(4)]

    def piece(side, g, k, arc, target):
        first = (side + 2 * (g // 2)) * TOK + (g % 2) * PART + k * CH
        rows = h0_ref.at[pl.ds(pl.multiple_of(first, CH), CH)]
        return pltpu.make_async_remote_copy(
            src_ref=rows, dst_ref=rows, send_sem=send.at[g, k, arc], recv_sem=recv.at[side, g, k],
            device_id=target, device_id_type=MESH,
        )

    def slot(s, _):
        for g in range(4):
            k = s - lags[g]

            @pl.when((k >= 0) & (k < NCH))
            def _():
                @pl.when((f != 0) | (b != core + 2 * (g // 2)))
                def _():
                    piece(core, g, k, 8, partner).wait_recv()

                for a in range(8):
                    if flags[g][a] is not None:
                        @pl.when(flags[g][a] == 1)
                        def _():
                            piece(core, g, k, a, targets[a]).start()

                piece(core, g, k, 8, partner).start()

        return 0

    lax.fori_loop(0, NCH + MAXLAG, slot, 0)

    def finish(k, _):
        for g in range(4):
            for a in range(8):
                if flags[g][a] is not None:
                    @pl.when(flags[g][a] == 1)
                    def _():
                        piece(core, g, k, a, targets[a]).wait_send()

            piece(core, g, k, 8, partner).wait_send()
            piece(1 - core, g, k, 8, partner).wait_recv()
        return 0

    lax.fori_loop(0, NCH, finish, 0)


def attend_kernel(h_ref, q_ref, h0_ref, wkv_ref, wout_ref, o_ref, keys, values, mix):
    lane = lax.broadcasted_iota(jnp.int32, (1, 128), 1)
    values[:, 128:] = jnp.ones((KEYS, 128), BF)
    block = 128

    @pl.loop(0, 5)
    def _(j):
        c = pl.multiple_of(j * 128, 128)
        w = jnp.concatenate([wkv_ref[:, pl.ds(c, 128)], wkv_ref[:, pl.ds(pl.multiple_of(C + c, 128), 128)]], axis=1)
        kv = jnp.dot(h0_ref[...], w, preferred_element_type=F32).astype(BF)
        keys[...] = kv[:, :128]
        values[:, :128] = kv[:, 128:]
        for half in range(2):
            keep = (lane < 64) if half == 0 else (lane >= 64)
            for r in range(TOK // block):
                rows = slice(r * block, (r + 1) * block)
                head = jnp.where(keep, q_ref[rows, pl.ds(c, 128)], jnp.zeros((), BF))
                scores = lax.dot_general(head, keys[...], (((1,), (1,)), ((), ())), preferred_element_type=F32)
                best = jnp.max(scores, axis=1, keepdims=True)
                prob = jnp.exp2(scores - best).astype(BF)
                out = jnp.dot(prob, values[...], preferred_element_type=F32)
                out = (out[:, :128] / out[:, 128:]).astype(BF)
                if half == 1:
                    out = jnp.where(keep, out, mix[rows, pl.ds(c, 128)])
                mix[rows, pl.ds(c, 128)] = out

    o_ref[...] = (
        h_ref[...].astype(F32) + jnp.dot(mix[...], wout_ref[...], preferred_element_type=F32)
    ).astype(BF)


def per_device(latents, conv_weight, conv_bias, w_query, w_keyval, w_out):
    vmem = pl.BlockSpec(memory_space=pltpu.VMEM)
    tokens = jax.ShapeDtypeStruct((TOK, C), BF)
    hidden, queries, first = pl.pallas_call(
        spread_kernel,
        out_shape=[tokens, tokens, jax.ShapeDtypeStruct((KEYS, C), BF)],
        in_specs=[vmem, pl.BlockSpec(memory_space=pl.ANY), vmem, vmem],
        out_specs=[vmem, vmem, vmem],
        scratch_shapes=[
            pltpu.VMEM((3, 3 * C, C), BF),
            pltpu.VMEM((3, TOK + 2 * COLS, C), BF),
            pltpu.VMEM((2, COLS, C), BF),
            pltpu.VMEM((TOK, C), F32),
            pltpu.SemaphoreType.DMA((3,)),
            pltpu.SemaphoreType.DMA((2,)),
            pltpu.SemaphoreType.DMA((2,)),
            pltpu.SemaphoreType.DMA((2, 4, NCH)),
            pltpu.SemaphoreType.DMA((4, NCH, 9)),
        ],
        compiler_params=pltpu.CompilerParams(collective_id=0, has_side_effects=True),
        name="spread",
    )(latents.reshape(TOK, C), conv_weight.reshape(3, 3 * C, C), conv_bias.reshape(1, C), w_query)
    result = pl.pallas_call(
        attend_kernel,
        out_shape=tokens,
        in_specs=[vmem] * 5,
        out_specs=vmem,
        scratch_shapes=[
            pltpu.VMEM((KEYS, 128), BF),
            pltpu.VMEM((KEYS, 256), BF),
            pltpu.VMEM((TOK, C), BF),
        ],
        name="attend",
    )(hidden, queries, first, w_keyval, w_out)
    return result.reshape(latents.shape)


def solution(mesh):
    return jax.shard_map(
        per_device,
        mesh=mesh,
        in_specs=(P("frame", "band", None, None), P(), P(), P(), P(), P()),
        out_specs=P("frame", "band", None, None),
        check_vma=False,
    )
```

```python
import jax
import jax.numpy as jnp
from jax import lax
from jax.experimental import pallas as pl
from jax.experimental.pallas import tpu as pltpu
from jax.sharding import PartitionSpec as P

BF = jnp.bfloat16
F32 = jnp.float32
MESH = pl.DeviceIdType.MESH
ROWS, COLS, C = 16, 32, 640
TOK = ROWS * COLS
KEYS = 4 * TOK
NCH = 8
PART = TOK // 2
CH = PART // NCH
SCALE = 0.125 * 1.4426950408889634

ARCS = (
    (
        (157049088, -1860284160, 0, 4),
        (92823553, 0, 2, 1860249119),
        (-2011160575, -1946156796, -2147483648, -2147454715),
        (-1929092543, 160064, 24576, 67133456),
        (201408768, 402718720, 16384, 83969292),
        (83914784, 88150272, 0, -2130706428),
        (16777216, 16777216, 0, 134217729),
        (4260096, 16384, 8192, 16384),
    ),
    (
        (1923194619, 1858111199, 0, 0),
        (-1337942274, 0, 0, -1878894304),
        (50406, 16896, 6176, 265216),
        (570425518, 402653325, 603979776, -2113929142),
        (8947727, 135170, 0, -2146955264),
        (-2113929023, 33280, 33685504, 164354),
        (131584, 0, 0, 0),
        (1073741824, 0, 0, 8388608),
    ),
    (
        (0, 0, -1188287234, -1281251928),
        (1073741824, 1280065620, -1226251028, 0),
        (24, 1050, 18398, 32960),
        (268435456, 33554432, -2013265684, 268435460),
        (128, -2071953280, -2147450868, 10520704),
        (263172, -2147483644, 69222597, 67372032),
        (0, 262148, 67108865, 0),
        (0, 0, 8388608, 0),
    ),
    (
        (0, 8224, 1112625921, 1279541328),
        (0, 867286947, 1090914817, 128),
        (2560, 1074043105, 1409318913, 100663840),
        (3072, 1627393058, 1392511489, 536871073),
        (1073741824, 1073741825, 1393821952, 33948160),
        (0, 268435489, 268470528, 268505585),
        (0, 1280, 66048, 0),
        (0, 1073741952, 1090519040, 1073741824),
    ),
)
LAGS = (
    ((0, 0, 0, 0), (1644203262, 1644171005, -536905953, 536903906), (1644201084, 301992000, 1879076992, 1342210146), (2178, 1610614461, -63713, 128), (0, 2, 35040, 0)),
    ((0, 0, 0, 0), (16843008, 73984, -16843011, 83960065), (208953344, 2088522796, 1567950110, 1549030428), (16843008, 74000, -16843011, 83960065), (0, 0, 16843008, 0)),
    ((0, 0, 0, 0), (-50529028, 50529027, 50529024, 1128465155), (289502477, 1648517666, 1112670720, 1107456514), (-318969632, 16843009, 16843008, 1094779137), (50529027, 0, 0, 0)),
    ((0, 0, 0, 0), (2013265907, -1946140596, -1474288388, 134219790), (1946440736, -2013265840, -1944051594, 204239900), (134212563, 67125260, 1164, 2062), (-2013265908, 0, 0, 0)),
)
MAXLAG = 20


STEPS = ((1, 0, 0), (-1, 0, 0), (0, 1, 0), (0, -1, 0), (0, 0, 1), (0, 0, -1), (0, 0, 2), (0, 0, -2))


def lookup(words, word, bit):
    value = jnp.int32(words[0])
    for k in range(1, 4):
        value = jnp.where(word == k, jnp.int32(words[k]), value)
    return lax.shift_right_logical(value, bit) & 1


def silu(v):
    v = v.astype(F32)
    return v * jax.nn.sigmoid(v)


def place(pad, act, row0):
    n = act.shape[0]
    rows = slice(row0, row0 + n)
    col = lax.broadcasted_iota(jnp.int32, (n, 1), 0) % COLS
    pad[rows, C : 2 * C] = act.astype(BF)
    pad[rows, 0:C] = jnp.where(col == 0, 0.0, pltpu.roll(act, 1, 0)).astype(BF)
    pad[rows, 2 * C :] = jnp.where(col == COLS - 1, 0.0, pltpu.roll(act, n - 1, 0)).astype(BF)


def block_kernel(
    x_hbm, w_hbm, b_ref, wq_hbm, wkv_hbm, wout_hbm, o_ref,
    x_ref, wbuf, wq_ref, wkv_ref, wout_ref, pad, halo, acc, hid_ref, q_ref, h0_ref, kv, mix,
    sems, hsend, hrecv, recv, send,
):
    f = lax.axis_index("frame")
    b = lax.axis_index("band")
    core = b % 2
    x = (b // 2) * 2 + f % 2
    y = f // 16
    z = (f // 2) % 8

    def chip(step):
        nx, ny, nz = (x + step[0] + 4) % 4, (y + step[1] + 4) % 4, (z + step[2] + 8) % 8
        return (ny * 16 + nz * 2 + nx % 2, (nx // 2) * 2 + core)

    targets = [chip(step) for step in STEPS]
    partner = (f, b + 1 - 2 * core)

    load_x = pltpu.make_async_copy(x_hbm, x_ref, sems.at[3])
    load_x.start()
    weights = [pltpu.make_async_copy(w_hbm.at[i], wbuf.at[i], sems.at[i]) for i in range(3)]
    for i in (1, 0, 2):
        weights[i].start()
    load_q = pltpu.make_async_copy(wq_hbm, wq_ref, sems.at[4])
    load_kv = pltpu.make_async_copy(wkv_hbm, wkv_ref, sems.at[5])
    load_out = pltpu.make_async_copy(wout_hbm, wout_ref, sems.at[6])
    for load in (load_q, load_kv, load_out):
        load.start()

    barrier = pltpu.get_barrier_semaphore()
    for target in targets + [partner]:
        pl.semaphore_signal(barrier, inc=1, device_id=target, device_id_type=MESH)
    middle = (b == 1) | (b == 2)

    @pl.when(middle)
    def _():
        pl.semaphore_signal(barrier, inc=1, device_id=(f, 3 - b), device_id_type=MESH)

    load_x.wait()
    place(pad, silu(x_ref[...]), COLS)
    pl.semaphore_wait(barrier, jnp.where(middle, 10, 9))

    def halo_copy(rows, slot, target):
        return pltpu.make_async_remote_copy(
            src_ref=x_ref.at[pl.ds(rows, COLS)], dst_ref=halo.at[slot],
            send_sem=hsend.at[slot], recv_sem=hrecv.at[slot],
            device_id=target, device_id_type=MESH,
        )

    up = halo_copy(0, 1, (f, jnp.maximum(b - 1, 0)))
    down = halo_copy(TOK - COLS, 0, (f, jnp.minimum(b + 1, 3)))

    @pl.when(b > 0)
    def _():
        up.start()

    @pl.when(b < 3)
    def _():
        down.start()

    weights[1].wait()
    acc[...] = (
        x_ref[...].astype(F32) + b_ref[...].astype(F32)
        + jnp.dot(pad[COLS : COLS + TOK], wbuf[1], preferred_element_type=F32)
    )

    @pl.when(b > 0)
    def _():
        up.wait_send()
        down.wait_recv()
        place(pad, silu(halo[0]), 0)

    @pl.when(b == 0)
    def _():
        pad[0:COLS] = jnp.zeros((COLS, 3 * C), BF)

    @pl.when(b < 3)
    def _():
        down.wait_send()
        up.wait_recv()
        place(pad, silu(halo[1]), TOK + COLS)

    @pl.when(b == 3)
    def _():
        pad[TOK + COLS :] = jnp.zeros((COLS, 3 * C), BF)

    weights[0].wait()
    weights[2].wait()
    hidden = (
        acc[...] + jnp.dot(pad[0:TOK], wbuf[0], preferred_element_type=F32)
        + jnp.dot(pad[2 * COLS :], wbuf[2], preferred_element_type=F32)
    ).astype(BF)
    hid_ref[...] = hidden

    @pl.when(f == 0)
    def _():
        h0_ref[pl.ds(pl.multiple_of(b * TOK, TOK), TOK), :] = hidden

    load_q.wait()
    q_ref[...] = (jnp.dot(hidden, wq_ref[...], preferred_element_type=F32) * SCALE).astype(BF)
    kv[:, :, 256:] = jnp.ones((5, KEYS, 128), BF)

    index = (x * 4 + y) * 8 + z
    word, bit = index // 32, index % 32
    flags = [[lookup(words, word, bit) if any(words) else None for words in ARCS[g]] for g in range(4)]
    lags = [sum(lookup(words, word, bit) * 2**i for i, words in enumerate(LAGS[g])) for g in range(4)]

    def piece(side, g, k, arc, target):
        first = (side + 2 * (g // 2)) * TOK + (g % 2) * PART + k * CH
        rows = h0_ref.at[pl.ds(pl.multiple_of(first, CH), CH)]
        return pltpu.make_async_remote_copy(
            src_ref=rows, dst_ref=rows, send_sem=send.at[g, k, arc], recv_sem=recv.at[side, g, k],
            device_id=target, device_id_type=MESH,
        )

    def slot(s, _):
        for g in range(4):
            k = s - lags[g]

            @pl.when((k >= 0) & (k < NCH))
            def _():
                @pl.when((f != 0) | (b != core + 2 * (g // 2)))
                def _():
                    piece(core, g, k, 8, partner).wait_recv()

                for a in range(8):
                    if flags[g][a] is not None:
                        @pl.when(flags[g][a] == 1)
                        def _():
                            piece(core, g, k, a, targets[a]).start()

                piece(core, g, k, 8, partner).start()

        return 0

    lax.fori_loop(0, NCH + MAXLAG, slot, 0)

    load_kv.wait()
    load_out.wait()

    def project(band):
        rows = pl.ds(pl.multiple_of(band * TOK, TOK), TOK)
        both = jnp.dot(h0_ref[rows, :], wkv_ref[...], preferred_element_type=F32).astype(BF)
        for j in range(5):
            kv[j, rows, 0:128] = both[:, j * 128 : (j + 1) * 128]
            kv[j, rows, 128:256] = both[:, C + j * 128 : C + (j + 1) * 128]

    def own(i, _):
        project(core + 2 * i)
        return 0

    lax.fori_loop(0, 2, own, 0)

    def other(i, _):
        def arrive(k, _):
            for h in range(2):
                piece(1 - core, 2 * i + h, k, 8, partner).wait_recv()
            return 0

        lax.fori_loop(0, NCH, arrive, 0)
        project(1 - core + 2 * i)
        return 0

    lax.fori_loop(0, 2, other, 0)

    lane = lax.broadcasted_iota(jnp.int32, (1, 128), 1)
    for j in range(5):
        columns = slice(j * 128, (j + 1) * 128)
        outs = []
        for half in range(2):
            keep = (lane < 64) if half == 0 else (lane >= 64)
            head = jnp.where(keep, q_ref[:, columns], jnp.zeros((), BF))
            scores = lax.dot_general(head, kv[j, :, 0:128], (((1,), (1,)), ((), ())), preferred_element_type=F32)
            best = jnp.max(scores, axis=1, keepdims=True)
            prob = jnp.exp2(scores - best).astype(BF)
            out = jnp.dot(prob, kv[j, :, 128:384], preferred_element_type=F32)
            outs.append(out[:, :128] / out[:, 128:])
        mix[:, columns] = jnp.where(lane < 64, outs[0], outs[1]).astype(BF)

    o_ref[...] = (
        hid_ref[...].astype(F32) + jnp.dot(mix[...], wout_ref[...], preferred_element_type=F32)
    ).astype(BF)

    def finish(k, _):
        for g in range(4):
            for a in range(8):
                if flags[g][a] is not None:
                    @pl.when(flags[g][a] == 1)
                    def _():
                        piece(core, g, k, a, targets[a]).wait_send()

            piece(core, g, k, 8, partner).wait_send()
        return 0

    lax.fori_loop(0, NCH, finish, 0)


def per_device(latents, conv_weight, conv_bias, w_query, w_keyval, w_out):
    vmem = pl.BlockSpec(memory_space=pltpu.VMEM)
    hbm = pl.BlockSpec(memory_space=pl.ANY)
    result = pl.pallas_call(
        block_kernel,
        out_shape=jax.ShapeDtypeStruct((TOK, C), BF),
        in_specs=[hbm, hbm, vmem, hbm, hbm, hbm],
        out_specs=vmem,
        scratch_shapes=[
            pltpu.VMEM((TOK, C), BF),
            pltpu.VMEM((3, 3 * C, C), BF),
            pltpu.VMEM((C, C), BF),
            pltpu.VMEM((C, 2 * C), BF),
            pltpu.VMEM((C, C), BF),
            pltpu.VMEM((TOK + 2 * COLS, 3 * C), BF),
            pltpu.VMEM((2, COLS, C), BF),
            pltpu.VMEM((TOK, C), F32),
            pltpu.VMEM((TOK, C), BF),
            pltpu.VMEM((TOK, C), BF),
            pltpu.VMEM((KEYS, C), BF),
            pltpu.VMEM((5, KEYS, 384), BF),
            pltpu.VMEM((TOK, C), BF),
            pltpu.SemaphoreType.DMA((7,)),
            pltpu.SemaphoreType.DMA((2,)),
            pltpu.SemaphoreType.DMA((2,)),
            pltpu.SemaphoreType.DMA((2, 4, NCH)),
            pltpu.SemaphoreType.DMA((4, NCH, 9)),
        ],
        compiler_params=pltpu.CompilerParams(collective_id=0, has_side_effects=True),
        name="block",
    )(latents.reshape(TOK, C), conv_weight.reshape(3, 3 * C, C), conv_bias, w_query, w_keyval, w_out)
    return result.reshape(latents.shape)


def solution(mesh):
    return jax.shard_map(
        per_device,
        mesh=mesh,
        in_specs=(P("frame", "band", None, None), P(), P(), P(), P(), P()),
        out_specs=P("frame", "band", None, None),
        check_vma=False,
    )
```

```python
import functools

import jax
import jax.numpy as jnp
from jax import lax
from jax.experimental import pallas as pl
from jax.experimental.pallas import tpu as pltpu
from jax.sharding import PartitionSpec as P

BF = jnp.bfloat16
F32 = jnp.float32
MESH = pl.DeviceIdType.MESH
ROWS, COLS, C = 16, 32, 640
TOK = ROWS * COLS
KEYS = 4 * TOK
NT = 2
NCH = 8
HALF = NCH // 2
PART = TOK // 4
CH = PART // HALF
SCALE = 0.125 * 1.4426950408889634

STEPS = (
    (1, 0, 0),
    (-1, 0, 0),
    (0, 1, 0),
    (0, -1, 0),
    (0, 0, 1),
    (0, 0, -1),
    (0, 0, 2),
    (0, 0, -2),
)
ARCS = (
    (
        (157049088, -1860284160, 0, 4),
        (92823553, 0, 2, 1860249119),
        (-2011160575, -1946156796, -2147483648, -2147454715),
        (-1929092543, 160064, 24576, 67133456),
        (201408768, 402718720, 16384, 83969292),
        (83914784, 88150272, 0, -2130706428),
        (16777216, 16777216, 0, 134217729),
        (4260096, 16384, 8192, 16384),
    ),
    (
        (1923194619, 1858111199, 0, 0),
        (-1337942274, 0, 0, -1878894304),
        (50406, 16896, 6176, 265216),
        (570425518, 402653325, 603979776, -2113929142),
        (8947727, 135170, 0, -2146955264),
        (-2113929023, 33280, 33685504, 164354),
        (131584, 0, 0, 0),
        (1073741824, 0, 0, 8388608),
    ),
    (
        (0, 0, -1188287234, -1281251928),
        (1073741824, 1280065620, -1226251028, 0),
        (24, 1050, 18398, 32960),
        (268435456, 33554432, -2013265684, 268435460),
        (128, -2071953280, -2147450868, 10520704),
        (263172, -2147483644, 69222597, 67372032),
        (0, 262148, 67108865, 0),
        (0, 0, 8388608, 0),
    ),
    (
        (0, 8224, 1112625921, 1279541328),
        (0, 867286947, 1090914817, 128),
        (2560, 1074043105, 1409318913, 100663840),
        (3072, 1627393058, 1392511489, 536871073),
        (1073741824, 1073741825, 1393821952, 33948160),
        (0, 268435489, 268470528, 268505585),
        (0, 1280, 66048, 0),
        (0, 1073741952, 1090519040, 1073741824),
    ),
)
LAGS = (
    ((0, 0, 0, 0), (1644203262, 1644171005, -536905953, 536903906), (1644201084, 301992000, 1879076992, 1342210146), (2178, 1610614461, -63713, 128), (0, 2, 35040, 0)),
    ((0, 0, 0, 0), (16843008, 73984, -16843011, 83960065), (208953344, 2088522796, 1567950110, 1549030428), (16843008, 74000, -16843011, 83960065), (0, 0, 16843008, 0)),
    ((0, 0, 0, 0), (-50529028, 50529027, 50529024, 1128465155), (289502477, 1648517666, 1112670720, 1107456514), (-318969632, 16843009, 16843008, 1094779137), (50529027, 0, 0, 0)),
    ((0, 0, 0, 0), (2013265907, -1946140596, -1474288388, 134219790), (1946440736, -2013265840, -1944051594, 204239900), (134212563, 67125260, 1164, 2062), (-2013265908, 0, 0, 0)),
)
MAXLAG = 20


def lookup(words, word, bit):
    value = jnp.int32(words[0])
    for k in range(1, 4):
        value = jnp.where(word == k, jnp.int32(words[k]), value)
    return lax.shift_right_logical(value, bit) & 1


def silu(v):
    v = v.astype(F32)
    return v * jax.nn.sigmoid(v)


def place(pad, act, row0):
    n = act.shape[0]
    rows = slice(row0, row0 + n)
    col = lax.broadcasted_iota(jnp.int32, (n, 1), 0) % COLS
    pad[rows, C : 2 * C] = act.astype(BF)
    pad[rows, 0:C] = jnp.where(col == 0, 0.0, pltpu.roll(act, 1, 0)).astype(BF)
    pad[rows, 2 * C :] = jnp.where(col == COLS - 1, 0.0, pltpu.roll(act, n - 1, 0)).astype(BF)


def block_kernel(
    x_hbm, w_hbm, b_ref, wq_hbm, wkv_hbm, wout_hbm, o_ref,
    x_ref, wbuf, wq_ref, wkv_ref, wout_ref, pad, halo, acc, hid_ref, q_ref, h0_ref, kv, mix,
    sems, hsend, hrecv, recv, send, psend, precv,
):
    f = lax.axis_index("frame")
    b = lax.axis_index("band")
    core = b % 2
    x = (b // 2) * 2 + f % 2
    y = f // 16
    z = (f // 2) % 8

    def chip(step):
        nx, ny, nz = (x + step[0] + 4) % 4, (y + step[1] + 4) % 4, (z + step[2] + 8) % 8
        return (ny * 16 + nz * 2 + nx % 2, (nx // 2) * 2 + core)

    targets = [chip(step) for step in STEPS]
    partner = (f, b + 1 - 2 * core)

    load_x = pltpu.make_async_copy(x_hbm, x_ref, sems.at[3])
    load_x.start()
    weights = [pltpu.make_async_copy(w_hbm.at[i], wbuf.at[i], sems.at[i]) for i in range(3)]
    for i in (1, 0, 2):
        weights[i].start()
    load_q = pltpu.make_async_copy(wq_hbm, wq_ref, sems.at[4])
    load_kv = pltpu.make_async_copy(wkv_hbm, wkv_ref, sems.at[5])
    load_out = pltpu.make_async_copy(wout_hbm, wout_ref, sems.at[6])
    for load in (load_q, load_kv, load_out):
        load.start()

    barrier = pltpu.get_barrier_semaphore()
    for target in targets + [partner]:
        pl.semaphore_signal(barrier, inc=1, device_id=target, device_id_type=MESH)
    middle = (b == 1) | (b == 2)

    @pl.when(middle)
    def _():
        pl.semaphore_signal(barrier, inc=1, device_id=(f, 3 - b), device_id_type=MESH)

    load_x.wait()
    place(pad, silu(x_ref[...]), COLS)
    pl.semaphore_wait(barrier, len(targets) + 1 + middle.astype(jnp.int32))

    def halo_copy(rows, slot, target):
        return pltpu.make_async_remote_copy(
            src_ref=x_ref.at[pl.ds(rows, COLS)], dst_ref=halo.at[slot],
            send_sem=hsend.at[slot], recv_sem=hrecv.at[slot],
            device_id=target, device_id_type=MESH,
        )

    up = halo_copy(0, 1, (f, jnp.maximum(b - 1, 0)))
    down = halo_copy(TOK - COLS, 0, (f, jnp.minimum(b + 1, 3)))

    @pl.when(b > 0)
    def _():
        up.start()

    @pl.when(b < 3)
    def _():
        down.start()

    weights[1].wait()
    acc[...] = (
        x_ref[...].astype(F32) + b_ref[...].astype(F32)
        + jnp.dot(pad[COLS : COLS + TOK], wbuf[1], preferred_element_type=F32)
    )

    @pl.when(b > 0)
    def _():
        up.wait_send()
        down.wait_recv()
        place(pad, silu(halo[0]), 0)

    @pl.when(b == 0)
    def _():
        pad[0:COLS] = jnp.zeros((COLS, 3 * C), BF)

    @pl.when(b < 3)
    def _():
        down.wait_send()
        up.wait_recv()
        place(pad, silu(halo[1]), TOK + COLS)

    @pl.when(b == 3)
    def _():
        pad[TOK + COLS :] = jnp.zeros((COLS, 3 * C), BF)

    index = (x * 4 + y) * 8 + z
    word, bit = index // 32, index % 32
    flags = [[lookup(words, word, bit) if any(words) else None for words in ARCS[g]] for g in range(2 * NT)]
    lags = [sum(lookup(words, word, bit) * 2**i for i, words in enumerate(LAGS[g])) for g in range(2 * NT)]

    def part_row(side, g, half):
        return (side + 2 * lax.div(g, NT)) * TOK + half * (2 * PART) + lax.rem(g, NT) * PART

    def piece(side, g, k, arc, target):
        first = part_row(side, g, lax.div(k, HALF)) + lax.rem(k, HALF) * CH
        rows = h0_ref.at[pl.ds(pl.multiple_of(first, CH), CH)]
        return pltpu.make_async_remote_copy(
            src_ref=rows, dst_ref=rows, send_sem=send.at[g, k, arc], recv_sem=recv.at[g, k],
            device_id=target, device_id_type=MESH,
        )

    def share(side, g, half):
        rows = h0_ref.at[pl.ds(pl.multiple_of(part_row(side, g, half), PART), PART)]
        return pltpu.make_async_remote_copy(
            src_ref=rows, dst_ref=rows, send_sem=psend.at[g, half], recv_sem=precv.at[g, half],
            device_id=partner, device_id_type=MESH,
        )

    def forward(g, k):
        for a in range(len(STEPS)):
            if flags[g][a] is not None:
                @pl.when(flags[g][a] == 1)
                def _():
                    piece(core, g, k, a, targets[a]).start()

        for half in range(2):
            @pl.when(k == half * HALF + HALF - 1)
            def _():
                share(core, g, half).start()

    def early(i):
        def send_one(k, _):
            for h in range(NT):
                forward(NT * i + h, k)
            return 0

        lax.fori_loop(0, HALF, send_one, 0)

    weights[0].wait()
    weights[2].wait()
    block = TOK // 2
    for half in range(2):
        top = half * block
        rows = slice(top, top + block)
        hidden = (
            acc[rows] + jnp.dot(pad[rows], wbuf[0], preferred_element_type=F32)
            + jnp.dot(pad[top + 2 * COLS : top + 2 * COLS + block], wbuf[2], preferred_element_type=F32)
        ).astype(BF)
        hid_ref[rows] = hidden

        @pl.when(f == 0)
        def _():
            h0_ref[pl.ds(pl.multiple_of(b * TOK + top, block), block), :] = hidden
            if half == 0:
                for i in range(2):
                    pl.when(b == core + 2 * i)(functools.partial(early, i))

    load_q.wait()

    def prepare():
        q_ref[...] = (jnp.dot(hid_ref[...], wq_ref[...], preferred_element_type=F32) * SCALE).astype(BF)
        kv[:, :, 256:] = jnp.ones((5, KEYS, 128), BF)

    pl.when(f != 0)(prepare)

    def slot(s, _):
        for g in range(2 * NT):
            k = s - lags[g]
            source = (f == 0) & (b == core + 2 * (g // NT))

            @pl.when((k >= 0) & (k < NCH) & jnp.logical_not(source & (k < HALF)))
            def _():
                @pl.when(jnp.logical_not(source))
                def _():
                    piece(core, g, k, 0, partner).wait_recv()

                forward(g, k)

        return 0

    lax.fori_loop(0, NCH + MAXLAG, slot, 0)

    pl.when(f == 0)(prepare)
    load_kv.wait()
    load_out.wait()

    def project(band):
        rows = pl.ds(pl.multiple_of(band * TOK, TOK), TOK)
        both = jnp.dot(h0_ref[rows, :], wkv_ref[...], preferred_element_type=F32).astype(BF)
        for j in range(5):
            kv[j, rows, 0:128] = both[:, j * 128 : (j + 1) * 128]
            kv[j, rows, 128:256] = both[:, C + j * 128 : C + (j + 1) * 128]

    def own(i, _):
        project(core + 2 * i)
        return 0

    lax.fori_loop(0, 2, own, 0)

    def other(i, _):
        for h in range(NT):
            for half in range(2):
                share(1 - core, NT * i + h, half).wait_recv()
        project(1 - core + 2 * i)
        return 0

    lax.fori_loop(0, 2, other, 0)

    lane = lax.broadcasted_iota(jnp.int32, (1, 128), 1)
    for j in range(5):
        columns = slice(j * 128, (j + 1) * 128)
        outs = []
        for half in range(2):
            keep = (lane < 64) if half == 0 else (lane >= 64)
            head = jnp.where(keep, q_ref[:, columns], jnp.zeros((), BF))
            scores = lax.dot_general(head, kv[j, :, 0:128], (((1,), (1,)), ((), ())), preferred_element_type=F32)
            best = jnp.max(scores, axis=1, keepdims=True)
            prob = jnp.exp2(scores - best).astype(BF)
            out = jnp.dot(prob, kv[j, :, 128:384], preferred_element_type=F32)
            outs.append(out[:, :128] / out[:, 128:])
        mix[:, columns] = jnp.where(lane < 64, outs[0], outs[1]).astype(BF)

    o_ref[...] = (
        hid_ref[...].astype(F32) + jnp.dot(mix[...], wout_ref[...], preferred_element_type=F32)
    ).astype(BF)

    def finish(k, _):
        for g in range(2 * NT):
            for a in range(len(STEPS)):
                if flags[g][a] is not None:
                    @pl.when(flags[g][a] == 1)
                    def _():
                        piece(core, g, k, a, targets[a]).wait_send()

        return 0

    lax.fori_loop(0, NCH, finish, 0)
    for g in range(2 * NT):
        for half in range(2):
            share(core, g, half).wait_send()


def per_device(latents, conv_weight, conv_bias, w_query, w_keyval, w_out):
    vmem = pl.BlockSpec(memory_space=pltpu.VMEM)
    hbm = pl.BlockSpec(memory_space=pl.ANY)
    result = pl.pallas_call(
        block_kernel,
        out_shape=jax.ShapeDtypeStruct((TOK, C), BF),
        in_specs=[hbm, hbm, vmem, hbm, hbm, hbm],
        out_specs=vmem,
        scratch_shapes=[
            pltpu.VMEM((TOK, C), BF),
            pltpu.VMEM((3, 3 * C, C), BF),
            pltpu.VMEM((C, C), BF),
            pltpu.VMEM((C, 2 * C), BF),
            pltpu.VMEM((C, C), BF),
            pltpu.VMEM((TOK + 2 * COLS, 3 * C), BF),
            pltpu.VMEM((2, COLS, C), BF),
            pltpu.VMEM((TOK, C), F32),
            pltpu.VMEM((TOK, C), BF),
            pltpu.VMEM((TOK, C), BF),
            pltpu.VMEM((KEYS, C), BF),
            pltpu.VMEM((5, KEYS, 384), BF),
            pltpu.VMEM((TOK, C), BF),
            pltpu.SemaphoreType.DMA((7,)),
            pltpu.SemaphoreType.DMA((2,)),
            pltpu.SemaphoreType.DMA((2,)),
            pltpu.SemaphoreType.DMA((2 * NT, NCH)),
            pltpu.SemaphoreType.DMA((2 * NT, NCH, len(STEPS))),
            pltpu.SemaphoreType.DMA((2 * NT, 2)),
            pltpu.SemaphoreType.DMA((2 * NT, 2)),
        ],
        compiler_params=pltpu.CompilerParams(collective_id=0, has_side_effects=True),
        name="block",
    )(latents.reshape(TOK, C), conv_weight.reshape(3, 3 * C, C), conv_bias, w_query, w_keyval, w_out)
    return result.reshape(latents.shape)


def solution(mesh):
    return jax.shard_map(
        per_device,
        mesh=mesh,
        in_specs=(P("frame", "band", None, None), P(), P(), P(), P(), P()),
        out_specs=P("frame", "band", None, None),
        check_vma=False,
    )
```

```python
import functools

import jax
import jax.numpy as jnp
from jax import lax
from jax.experimental import pallas as pl
from jax.experimental.pallas import tpu as pltpu
from jax.sharding import PartitionSpec as P

BF = jnp.bfloat16
F32 = jnp.float32
MESH = pl.DeviceIdType.MESH
ROWS, COLS, C = 16, 32, 640
TOK = ROWS * COLS
KEYS = 4 * TOK
NT = 2
NCH = 8
HALF = NCH // 2
DELTA = 2
PART = TOK // 4
CH = PART // HALF
SCALE = 0.125 * 1.4426950408889634

STEPS = (
    (1, 0, 0),
    (-1, 0, 0),
    (0, 1, 0),
    (0, -1, 0),
    (0, 0, 1),
    (0, 0, -1),
    (0, 0, 2),
    (0, 0, -2),
)
ARCS = (
    (
        (157049088, -1860284160, 0, 4),
        (92823553, 0, 2, 1860249119),
        (-2011160575, -1946156796, -2147483648, -2147454715),
        (-1929092543, 160064, 24576, 67133456),
        (201408768, 402718720, 16384, 83969292),
        (83914784, 88150272, 0, -2130706428),
        (16777216, 16777216, 0, 134217729),
        (4260096, 16384, 8192, 16384),
    ),
    (
        (1923194619, 1858111199, 0, 0),
        (-1337942274, 0, 0, -1878894304),
        (50406, 16896, 6176, 265216),
        (570425518, 402653325, 603979776, -2113929142),
        (8947727, 135170, 0, -2146955264),
        (-2113929023, 33280, 33685504, 164354),
        (131584, 0, 0, 0),
        (1073741824, 0, 0, 8388608),
    ),
    (
        (0, 0, -1188287234, -1281251928),
        (1073741824, 1280065620, -1226251028, 0),
        (24, 1050, 18398, 32960),
        (268435456, 33554432, -2013265684, 268435460),
        (128, -2071953280, -2147450868, 10520704),
        (263172, -2147483644, 69222597, 67372032),
        (0, 262148, 67108865, 0),
        (0, 0, 8388608, 0),
    ),
    (
        (0, 8224, 1112625921, 1279541328),
        (0, 867286947, 1090914817, 128),
        (2560, 1074043105, 1409318913, 100663840),
        (3072, 1627393058, 1392511489, 536871073),
        (1073741824, 1073741825, 1393821952, 33948160),
        (0, 268435489, 268470528, 268505585),
        (0, 1280, 66048, 0),
        (0, 1073741952, 1090519040, 1073741824),
    ),
)
LAGS = (
    ((0, 0, 0, 0), (1644203262, 1644171005, -536905953, 536903906), (1644201084, 301992000, 1879076992, 1342210146), (2178, 1610614461, -63713, 128), (0, 2, 35040, 0)),
    ((0, 0, 0, 0), (16843008, 73984, -16843011, 83960065), (208953344, 2088522796, 1567950110, 1549030428), (16843008, 74000, -16843011, 83960065), (0, 0, 16843008, 0)),
    ((0, 0, 0, 0), (-50529028, 50529027, 50529024, 1128465155), (289502477, 1648517666, 1112670720, 1107456514), (-318969632, 16843009, 16843008, 1094779137), (50529027, 0, 0, 0)),
    ((0, 0, 0, 0), (2013265907, -1946140596, -1474288388, 134219790), (1946440736, -2013265840, -1944051594, 204239900), (134212563, 67125260, 1164, 2062), (-2013265908, 0, 0, 0)),
)
MAXLAG = 20


def lookup(words, word, bit):
    value = jnp.int32(words[0])
    for k in range(1, 4):
        value = jnp.where(word == k, jnp.int32(words[k]), value)
    return lax.shift_right_logical(value, bit) & 1


def silu(v):
    v = v.astype(F32)
    return v * jax.nn.sigmoid(v)


def place(pad, act, row0):
    n = act.shape[0]
    rows = slice(row0, row0 + n)
    col = lax.broadcasted_iota(jnp.int32, (n, 1), 0) % COLS
    pad[rows, C : 2 * C] = act.astype(BF)
    pad[rows, 0:C] = jnp.where(col == 0, 0.0, pltpu.roll(act, 1, 0)).astype(BF)
    pad[rows, 2 * C :] = jnp.where(col == COLS - 1, 0.0, pltpu.roll(act, n - 1, 0)).astype(BF)


def block_kernel(
    x_ref, w_hbm, b_ref, wq_hbm, wkv_hbm, wout_hbm, o_ref,
    wbuf, wq_ref, wkv_ref, wout_ref, pad, halo, acc, hid_ref, q_ref, h0_ref, kv, mix,
    sems, hsend, hrecv, recv, send, psend, precv,
):
    f = lax.axis_index("frame")
    b = lax.axis_index("band")
    core = b % 2
    x = (b // 2) * 2 + f % 2
    y = f // 16
    z = (f // 2) % 8

    def chip(step):
        nx, ny, nz = (x + step[0] + 4) % 4, (y + step[1] + 4) % 4, (z + step[2] + 8) % 8
        return (ny * 16 + nz * 2 + nx % 2, (nx // 2) * 2 + core)

    targets = [chip(step) for step in STEPS]
    partner = (f, b + 1 - 2 * core)

    weights = [pltpu.make_async_copy(w_hbm.at[i], wbuf.at[i], sems.at[i]) for i in range(3)]
    for i in (1, 0, 2):
        weights[i].start()
    load_q = pltpu.make_async_copy(wq_hbm, wq_ref, sems.at[3])
    load_kv = pltpu.make_async_copy(wkv_hbm, wkv_ref, sems.at[4])
    load_out = pltpu.make_async_copy(wout_hbm, wout_ref, sems.at[5])
    for load in (load_q, load_kv, load_out):
        load.start()

    barrier = pltpu.get_barrier_semaphore()
    for target in targets + [partner]:
        pl.semaphore_signal(barrier, inc=1, device_id=target, device_id_type=MESH)
    middle = (b == 1) | (b == 2)

    @pl.when(middle)
    def _():
        pl.semaphore_signal(barrier, inc=1, device_id=(f, 3 - b), device_id_type=MESH)

    place(pad, silu(x_ref[...]), COLS)
    pl.semaphore_wait(barrier, len(targets) + 1 + middle.astype(jnp.int32))

    def halo_copy(rows, slot, target):
        return pltpu.make_async_remote_copy(
            src_ref=x_ref.at[pl.ds(rows, COLS)], dst_ref=halo.at[slot],
            send_sem=hsend.at[slot], recv_sem=hrecv.at[slot],
            device_id=target, device_id_type=MESH,
        )

    up = halo_copy(0, 1, (f, jnp.maximum(b - 1, 0)))
    down = halo_copy(TOK - COLS, 0, (f, jnp.minimum(b + 1, 3)))

    @pl.when(b > 0)
    def _():
        up.start()

    @pl.when(b < 3)
    def _():
        down.start()

    weights[1].wait()
    acc[...] = (
        x_ref[...].astype(F32) + b_ref[...].astype(F32)
        + jnp.dot(pad[COLS : COLS + TOK], wbuf[1], preferred_element_type=F32)
    )

    @pl.when(b > 0)
    def _():
        up.wait_send()
        down.wait_recv()
        place(pad, silu(halo[0]), 0)

    @pl.when(b == 0)
    def _():
        pad[0:COLS] = jnp.zeros((COLS, 3 * C), BF)

    @pl.when(b < 3)
    def _():
        down.wait_send()
        up.wait_recv()
        place(pad, silu(halo[1]), TOK + COLS)

    @pl.when(b == 3)
    def _():
        pad[TOK + COLS :] = jnp.zeros((COLS, 3 * C), BF)

    index = (x * 4 + y) * 8 + z
    word, bit = index // 32, index % 32
    flags = [[lookup(words, word, bit) if any(words) else None for words in ARCS[g]] for g in range(2 * NT)]
    lags = [sum(lookup(words, word, bit) * 2**i for i, words in enumerate(LAGS[g])) for g in range(2 * NT)]

    def part_row(side, g, half):
        return (side + 2 * lax.div(g, NT)) * TOK + half * (2 * PART) + lax.rem(g, NT) * PART

    def piece(side, g, k, arc, target):
        first = part_row(side, g, lax.div(k, HALF)) + lax.rem(k, HALF) * CH
        rows = h0_ref.at[pl.ds(pl.multiple_of(first, CH), CH)]
        return pltpu.make_async_remote_copy(
            src_ref=rows, dst_ref=rows, send_sem=send.at[g, k, arc], recv_sem=recv.at[g, k],
            device_id=target, device_id_type=MESH,
        )

    def share(side, g, half):
        rows = h0_ref.at[pl.ds(pl.multiple_of(part_row(side, g, half), PART), PART)]
        return pltpu.make_async_remote_copy(
            src_ref=rows, dst_ref=rows, send_sem=psend.at[g, half], recv_sem=precv.at[g, half],
            device_id=partner, device_id_type=MESH,
        )

    def forward(g, k):
        for a in range(len(STEPS)):
            if flags[g][a] is not None:
                @pl.when(flags[g][a] == 1)
                def _():
                    piece(core, g, k, a, targets[a]).start()

        for half in range(2):
            @pl.when(k == half * HALF + HALF - 1)
            def _():
                share(core, g, half).start()

    def early(i):
        def send_one(k, _):
            for h in range(NT):
                forward(NT * i + h, k)
            return 0

        lax.fori_loop(0, HALF, send_one, 0)

    weights[0].wait()
    weights[2].wait()
    block = TOK // 2
    for half in range(2):
        top = half * block
        rows = slice(top, top + block)
        hidden = (
            acc[rows] + jnp.dot(pad[rows], wbuf[0], preferred_element_type=F32)
            + jnp.dot(pad[top + 2 * COLS : top + 2 * COLS + block], wbuf[2], preferred_element_type=F32)
        ).astype(BF)
        hid_ref[rows] = hidden

        @pl.when(f == 0)
        def _():
            h0_ref[pl.ds(pl.multiple_of(b * TOK + top, block), block), :] = hidden
            if half == 0:
                for i in range(2):
                    pl.when(b == core + 2 * i)(functools.partial(early, i))

    load_q.wait()

    def prepare():
        q_ref[...] = (jnp.dot(hid_ref[...], wq_ref[...], preferred_element_type=F32) * SCALE).astype(BF)
        kv[:, :, 256:] = jnp.ones((5, KEYS, 128), BF)

    pl.when(f != 0)(prepare)

    load_kv.wait()

    def project(side, g):
        low, high = [pl.ds(pl.multiple_of(part_row(side, g, half), PART), PART) for half in range(2)]
        rows = jnp.concatenate([h0_ref[low, :], h0_ref[high, :]], axis=0)
        both = jnp.dot(rows, wkv_ref[...], preferred_element_type=F32).astype(BF)
        for j in range(5):
            pair = jnp.concatenate([both[:, j * 128 : (j + 1) * 128], both[:, C + j * 128 : C + (j + 1) * 128]], axis=1)
            kv[j, low, 0:256] = pair[:PART]
            kv[j, high, 0:256] = pair[PART:]

    def slot(s, _):
        for g in range(2 * NT):
            k = s - lags[g]
            source = (f == 0) & (b == core + 2 * (g // NT))

            @pl.when((k >= 0) & (k < NCH) & jnp.logical_not(source & (k < HALF)))
            def _():
                @pl.when(jnp.logical_not(source))
                def _():
                    piece(core, g, k, 0, partner).wait_recv()

                forward(g, k)

        ends = [s - lags[g] - NCH for g in range(2 * NT)]
        due = sum((e == -1).astype(jnp.int32) + (e == DELTA).astype(jnp.int32) for e in ends)

        @pl.when(due > 0)
        def _():
            def one(t, _):
                g = lax.rem(t, 2 * NT)
                late = t >= 2 * NT
                end = ends[0]
                for h in range(1, 2 * NT):
                    end = jnp.where(g == h, ends[h], end)

                @pl.when(end == jnp.where(late, DELTA, -1))
                def _():
                    @pl.when(late)
                    def _():
                        for half in range(2):
                            share(1 - core, g, half).wait_recv()

                    project(jnp.where(late, 1 - core, core), g)

                return 0

            lax.fori_loop(0, 4 * NT, one, 0)

        return 0

    lax.fori_loop(0, NCH + MAXLAG + DELTA + 1, slot, 0)

    pl.when(f == 0)(prepare)
    load_out.wait()

    lane = lax.broadcasted_iota(jnp.int32, (1, 128), 1)
    for j in range(5):
        columns = slice(j * 128, (j + 1) * 128)
        outs = []
        for half in range(2):
            keep = (lane < 64) if half == 0 else (lane >= 64)
            head = jnp.where(keep, q_ref[:, columns], jnp.zeros((), BF))
            scores = lax.dot_general(head, kv[j, :, 0:128], (((1,), (1,)), ((), ())), preferred_element_type=F32)
            best = jnp.max(scores, axis=1, keepdims=True)
            prob = jnp.exp2(scores - best).astype(BF)
            out = jnp.dot(prob, kv[j, :, 128:384], preferred_element_type=F32)
            outs.append(out[:, :128] / out[:, 128:])
        mix[:, columns] = jnp.where(lane < 64, outs[0], outs[1]).astype(BF)

    o_ref[...] = (
        hid_ref[...].astype(F32) + jnp.dot(mix[...], wout_ref[...], preferred_element_type=F32)
    ).astype(BF)

    def finish(k, _):
        for g in range(2 * NT):
            for a in range(len(STEPS)):
                if flags[g][a] is not None:
                    @pl.when(flags[g][a] == 1)
                    def _():
                        piece(core, g, k, a, targets[a]).wait_send()

        return 0

    lax.fori_loop(0, NCH, finish, 0)
    for g in range(2 * NT):
        for half in range(2):
            share(core, g, half).wait_send()


def per_device(latents, conv_weight, conv_bias, w_query, w_keyval, w_out):
    vmem = pl.BlockSpec(memory_space=pltpu.VMEM)
    hbm = pl.BlockSpec(memory_space=pl.ANY)
    result = pl.pallas_call(
        block_kernel,
        out_shape=jax.ShapeDtypeStruct((TOK, C), BF),
        in_specs=[vmem, hbm, vmem, hbm, hbm, hbm],
        out_specs=vmem,
        scratch_shapes=[
            pltpu.VMEM((3, 3 * C, C), BF),
            pltpu.VMEM((C, C), BF),
            pltpu.VMEM((C, 2 * C), BF),
            pltpu.VMEM((C, C), BF),
            pltpu.VMEM((TOK + 2 * COLS, 3 * C), BF),
            pltpu.VMEM((2, COLS, C), BF),
            pltpu.VMEM((TOK, C), F32),
            pltpu.VMEM((TOK, C), BF),
            pltpu.VMEM((TOK, C), BF),
            pltpu.VMEM((KEYS, C), BF),
            pltpu.VMEM((5, KEYS, 384), BF),
            pltpu.VMEM((TOK, C), BF),
            pltpu.SemaphoreType.DMA((6,)),
            pltpu.SemaphoreType.DMA((2,)),
            pltpu.SemaphoreType.DMA((2,)),
            pltpu.SemaphoreType.DMA((2 * NT, NCH)),
            pltpu.SemaphoreType.DMA((2 * NT, NCH, len(STEPS))),
            pltpu.SemaphoreType.DMA((2 * NT, 2)),
            pltpu.SemaphoreType.DMA((2 * NT, 2)),
        ],
        compiler_params=pltpu.CompilerParams(collective_id=0, has_side_effects=True, vmem_limit_bytes=52 << 20),
        name="block",
    )(latents.reshape(TOK, C), conv_weight.reshape(3, 3 * C, C), conv_bias, w_query, w_keyval, w_out)
    return result.reshape(latents.shape)


def solution(mesh):
    return jax.shard_map(
        per_device,
        mesh=mesh,
        in_specs=(P("frame", "band", None, None), P(), P(), P(), P(), P()),
        out_specs=P("frame", "band", None, None),
        check_vma=False,
    )
```

```python
import functools

import jax
import jax.numpy as jnp
from jax import lax
from jax.experimental import pallas as pl
from jax.experimental.pallas import tpu as pltpu
from jax.sharding import PartitionSpec as P

BF = jnp.bfloat16
F32 = jnp.float32
MESH = pl.DeviceIdType.MESH
ROWS, COLS, C = 16, 32, 640
TOK = ROWS * COLS
KEYS = 4 * TOK
NT = 2
NCH = 8
HALF = NCH // 2
DELTA = 2
PART = TOK // 4
CH = PART // HALF
SCALE = 0.125 * 1.4426950408889634

STEPS = (
    (1, 0, 0),
    (-1, 0, 0),
    (0, 1, 0),
    (0, -1, 0),
    (0, 0, 1),
    (0, 0, -1),
    (0, 0, 2),
    (0, 0, -2),
)
ARCS = (
    (
        (157049088, -1860284160, 0, 4),
        (92823553, 0, 2, 1860249119),
        (-2011160575, -1946156796, -2147483648, -2147454715),
        (-1929092543, 160064, 24576, 67133456),
        (201408768, 402718720, 16384, 83969292),
        (83914784, 88150272, 0, -2130706428),
        (16777216, 16777216, 0, 134217729),
        (4260096, 16384, 8192, 16384),
    ),
    (
        (1923194619, 1858111199, 0, 0),
        (-1337942274, 0, 0, -1878894304),
        (50406, 16896, 6176, 265216),
        (570425518, 402653325, 603979776, -2113929142),
        (8947727, 135170, 0, -2146955264),
        (-2113929023, 33280, 33685504, 164354),
        (131584, 0, 0, 0),
        (1073741824, 0, 0, 8388608),
    ),
    (
        (0, 0, -1188287234, -1281251928),
        (1073741824, 1280065620, -1226251028, 0),
        (24, 1050, 18398, 32960),
        (268435456, 33554432, -2013265684, 268435460),
        (128, -2071953280, -2147450868, 10520704),
        (263172, -2147483644, 69222597, 67372032),
        (0, 262148, 67108865, 0),
        (0, 0, 8388608, 0),
    ),
    (
        (0, 8224, 1112625921, 1279541328),
        (0, 867286947, 1090914817, 128),
        (2560, 1074043105, 1409318913, 100663840),
        (3072, 1627393058, 1392511489, 536871073),
        (1073741824, 1073741825, 1393821952, 33948160),
        (0, 268435489, 268470528, 268505585),
        (0, 1280, 66048, 0),
        (0, 1073741952, 1090519040, 1073741824),
    ),
)
LAGS = (
    ((0, 0, 0, 0), (1644203262, 1644171005, -536905953, 536903906), (1644201084, 301992000, 1879076992, 1342210146), (2178, 1610614461, -63713, 128), (0, 2, 35040, 0)),
    ((0, 0, 0, 0), (16843008, 73984, -16843011, 83960065), (208953344, 2088522796, 1567950110, 1549030428), (16843008, 74000, -16843011, 83960065), (0, 0, 16843008, 0)),
    ((0, 0, 0, 0), (-50529028, 50529027, 50529024, 1128465155), (289502477, 1648517666, 1112670720, 1107456514), (-318969632, 16843009, 16843008, 1094779137), (50529027, 0, 0, 0)),
    ((0, 0, 0, 0), (2013265907, -1946140596, -1474288388, 134219790), (1946440736, -2013265840, -1944051594, 204239900), (134212563, 67125260, 1164, 2062), (-2013265908, 0, 0, 0)),
)
MAXLAG = 20


def lookup(words, word, bit):
    value = jnp.int32(words[0])
    for k in range(1, 4):
        value = jnp.where(word == k, jnp.int32(words[k]), value)
    return lax.shift_right_logical(value, bit) & 1


def silu(v):
    v = v.astype(F32)
    return v * jax.nn.sigmoid(v)


def place(pad, act, row0):
    n = act.shape[0]
    rows = slice(row0, row0 + n)
    col = lax.broadcasted_iota(jnp.int32, (n, 1), 0) % COLS
    pad[rows, C : 2 * C] = act.astype(BF)
    pad[rows, 0:C] = jnp.where(col == 0, 0.0, pltpu.roll(act, 1, 0)).astype(BF)
    pad[rows, 2 * C :] = jnp.where(col == COLS - 1, 0.0, pltpu.roll(act, n - 1, 0)).astype(BF)


def block_kernel(
    x_ref, w_hbm, b_ref, wq_hbm, wkv_hbm, wout_hbm, o_ref,
    wbuf, wq_ref, wkv_ref, wout_ref, pad, halo, acc, hid_ref, q_ref, h0_ref, kv, mix,
    sems, hsend, hrecv, recv, send, psend, precv,
):
    f = lax.axis_index("frame")
    b = lax.axis_index("band")
    core = b % 2
    x = (b // 2) * 2 + f % 2
    y = f // 16
    z = (f // 2) % 8

    def chip(step):
        nx, ny, nz = (x + step[0] + 4) % 4, (y + step[1] + 4) % 4, (z + step[2] + 8) % 8
        return (ny * 16 + nz * 2 + nx % 2, (nx // 2) * 2 + core)

    targets = [chip(step) for step in STEPS]
    partner = (f, b + 1 - 2 * core)

    weights = [pltpu.make_async_copy(w_hbm.at[i], wbuf.at[i], sems.at[i]) for i in range(3)]
    for i in (1, 0, 2):
        weights[i].start()
    load_q = pltpu.make_async_copy(wq_hbm, wq_ref, sems.at[3])
    load_kv = pltpu.make_async_copy(wkv_hbm, wkv_ref, sems.at[4])
    load_out = pltpu.make_async_copy(wout_hbm, wout_ref, sems.at[5])
    for load in (load_q, load_kv, load_out):
        load.start()

    barrier = pltpu.get_barrier_semaphore()
    for target in targets + [partner]:
        pl.semaphore_signal(barrier, inc=1, device_id=target, device_id_type=MESH)
    middle = (b == 1) | (b == 2)

    @pl.when(middle)
    def _():
        pl.semaphore_signal(barrier, inc=1, device_id=(f, 3 - b), device_id_type=MESH)

    place(pad, silu(x_ref[...]), COLS)
    pl.semaphore_wait(barrier, len(targets) + 1 + middle.astype(jnp.int32))

    def halo_copy(rows, slot, target):
        return pltpu.make_async_remote_copy(
            src_ref=x_ref.at[pl.ds(rows, COLS)], dst_ref=halo.at[slot],
            send_sem=hsend.at[slot], recv_sem=hrecv.at[slot],
            device_id=target, device_id_type=MESH,
        )

    up = halo_copy(0, 1, (f, jnp.maximum(b - 1, 0)))
    down = halo_copy(TOK - COLS, 0, (f, jnp.minimum(b + 1, 3)))

    @pl.when(b > 0)
    def _():
        up.start()

    @pl.when(b < 3)
    def _():
        down.start()

    weights[1].wait()
    acc[...] = (
        x_ref[...].astype(F32) + b_ref[...].astype(F32)
        + jnp.dot(pad[COLS : COLS + TOK], wbuf[1], preferred_element_type=F32)
    )

    @pl.when(b > 0)
    def _():
        up.wait_send()
        down.wait_recv()
        place(pad, silu(halo[0]), 0)

    @pl.when(b == 0)
    def _():
        pad[0:COLS] = jnp.zeros((COLS, 3 * C), BF)

    @pl.when(b < 3)
    def _():
        down.wait_send()
        up.wait_recv()
        place(pad, silu(halo[1]), TOK + COLS)

    @pl.when(b == 3)
    def _():
        pad[TOK + COLS :] = jnp.zeros((COLS, 3 * C), BF)

    index = (x * 4 + y) * 8 + z
    word, bit = index // 32, index % 32
    flags = [[lookup(words, word, bit) if any(words) else None for words in ARCS[g]] for g in range(2 * NT)]
    lags = [sum(lookup(words, word, bit) * 2**i for i, words in enumerate(LAGS[g])) for g in range(2 * NT)]

    def part_row(side, g, half):
        return (side + 2 * lax.div(g, NT)) * TOK + half * (2 * PART) + lax.rem(g, NT) * PART

    def piece(side, g, k, arc, target):
        first = part_row(side, g, lax.div(k, HALF)) + lax.rem(k, HALF) * CH
        rows = h0_ref.at[pl.ds(pl.multiple_of(first, CH), CH)]
        return pltpu.make_async_remote_copy(
            src_ref=rows, dst_ref=rows, send_sem=send.at[g, arc], recv_sem=recv.at[g, k],
            device_id=target, device_id_type=MESH,
        )

    def share(side, g, half):
        rows = h0_ref.at[pl.ds(pl.multiple_of(part_row(side, g, half), PART), PART)]
        return pltpu.make_async_remote_copy(
            src_ref=rows, dst_ref=rows, send_sem=psend.at[g, half], recv_sem=precv.at[g, half],
            device_id=partner, device_id_type=MESH,
        )

    def forward(g, k):
        for a in range(len(STEPS)):
            if flags[g][a] is not None:
                @pl.when(flags[g][a] == 1)
                def _():
                    piece(core, g, k, a, targets[a]).start()

        for half in range(2):
            @pl.when(k == half * HALF + HALF - 1)
            def _():
                share(core, g, half).start()

    def early(i):
        def send_one(k, _):
            for h in range(NT):
                forward(NT * i + h, k)
            return 0

        lax.fori_loop(0, HALF, send_one, 0)

    weights[0].wait()
    weights[2].wait()
    block = TOK // 2
    for half in range(2):
        top = half * block
        rows = slice(top, top + block)
        hidden = (
            acc[rows] + jnp.dot(pad[rows], wbuf[0], preferred_element_type=F32)
            + jnp.dot(pad[top + 2 * COLS : top + 2 * COLS + block], wbuf[2], preferred_element_type=F32)
        ).astype(BF)
        hid_ref[rows] = hidden

        @pl.when(f == 0)
        def _():
            h0_ref[pl.ds(pl.multiple_of(b * TOK + top, block), block), :] = hidden
            if half == 0:
                for i in range(2):
                    pl.when(b == core + 2 * i)(functools.partial(early, i))

    load_q.wait()

    def prepare():
        q_ref[...] = (jnp.dot(hid_ref[...], wq_ref[...], preferred_element_type=F32) * SCALE).astype(BF)
        kv[:, :, 256:] = jnp.ones((5, KEYS, 128), BF)

    pl.when(f != 0)(prepare)

    load_kv.wait()

    def project(side, g):
        low, high = [pl.ds(pl.multiple_of(part_row(side, g, half), PART), PART) for half in range(2)]
        rows = jnp.concatenate([h0_ref[low, :], h0_ref[high, :]], axis=0)
        both = jnp.dot(rows, wkv_ref[...], preferred_element_type=F32).astype(BF)
        for j in range(5):
            pair = jnp.concatenate([both[:, j * 128 : (j + 1) * 128], both[:, C + j * 128 : C + (j + 1) * 128]], axis=1)
            kv[j, low, 0:256] = pair[:PART]
            kv[j, high, 0:256] = pair[PART:]

    def slot(s, _):
        for g in range(2 * NT):
            k = s - lags[g]
            source = (f == 0) & (b == core + 2 * (g // NT))

            @pl.when((k >= 0) & (k < NCH) & jnp.logical_not(source & (k < HALF)))
            def _():
                @pl.when(jnp.logical_not(source))
                def _():
                    piece(core, g, k, 0, partner).wait_recv()

                forward(g, k)

        ends = [s - lags[g] - NCH for g in range(2 * NT)]
        due = sum((e == -1).astype(jnp.int32) + (e == DELTA).astype(jnp.int32) for e in ends)

        @pl.when(due > 0)
        def _():
            def one(t, _):
                g = lax.rem(t, 2 * NT)
                late = t >= 2 * NT
                end = ends[0]
                for h in range(1, 2 * NT):
                    end = jnp.where(g == h, ends[h], end)

                @pl.when(end == jnp.where(late, DELTA, -1))
                def _():
                    @pl.when(late)
                    def _():
                        for half in range(2):
                            share(1 - core, g, half).wait_recv()

                    project(jnp.where(late, 1 - core, core), g)

                return 0

            lax.fori_loop(0, 4 * NT, one, 0)

        return 0

    lax.fori_loop(0, NCH + MAXLAG + DELTA + 1, slot, 0)

    pl.when(f == 0)(prepare)
    load_out.wait()

    lane = lax.broadcasted_iota(jnp.int32, (1, 128), 1)
    for j in range(5):
        columns = slice(j * 128, (j + 1) * 128)
        outs = []
        for half in range(2):
            keep = (lane < 64) if half == 0 else (lane >= 64)
            head = jnp.where(keep, q_ref[:, columns], jnp.zeros((), BF))
            scores = lax.dot_general(head, kv[j, :, 0:128], (((1,), (1,)), ((), ())), preferred_element_type=F32)
            best = jnp.max(scores, axis=1, keepdims=True)
            prob = jnp.exp2(scores - best).astype(BF)
            out = jnp.dot(prob, kv[j, :, 128:384], preferred_element_type=F32)
            outs.append(out[:, :128] / out[:, 128:])
        mix[:, columns] = jnp.where(lane < 64, outs[0], outs[1]).astype(BF)

    o_ref[...] = (
        hid_ref[...].astype(F32) + jnp.dot(mix[...], wout_ref[...], preferred_element_type=F32)
    ).astype(BF)

    whole = h0_ref.at[pl.ds(0, 2 * PART)]
    for g in range(2 * NT):
        for a in range(len(STEPS)):
            if flags[g][a] is not None:
                @pl.when(flags[g][a] == 1)
                def _():
                    pltpu.make_async_remote_copy(
                        src_ref=whole, dst_ref=whole, send_sem=send.at[g, a], recv_sem=recv.at[g, 0],
                        device_id=targets[a], device_id_type=MESH,
                    ).wait_send()

    for g in range(2 * NT):
        for half in range(2):
            share(core, g, half).wait_send()


def per_device(latents, conv_weight, conv_bias, w_query, w_keyval, w_out):
    vmem = pl.BlockSpec(memory_space=pltpu.VMEM)
    hbm = pl.BlockSpec(memory_space=pl.ANY)
    result = pl.pallas_call(
        block_kernel,
        out_shape=jax.ShapeDtypeStruct((TOK, C), BF),
        in_specs=[vmem, hbm, vmem, hbm, hbm, hbm],
        out_specs=vmem,
        scratch_shapes=[
            pltpu.VMEM((3, 3 * C, C), BF),
            pltpu.VMEM((C, C), BF),
            pltpu.VMEM((C, 2 * C), BF),
            pltpu.VMEM((C, C), BF),
            pltpu.VMEM((TOK + 2 * COLS, 3 * C), BF),
            pltpu.VMEM((2, COLS, C), BF),
            pltpu.VMEM((TOK, C), F32),
            pltpu.VMEM((TOK, C), BF),
            pltpu.VMEM((TOK, C), BF),
            pltpu.VMEM((KEYS, C), BF),
            pltpu.VMEM((5, KEYS, 384), BF),
            pltpu.VMEM((TOK, C), BF),
            pltpu.SemaphoreType.DMA((6,)),
            pltpu.SemaphoreType.DMA((2,)),
            pltpu.SemaphoreType.DMA((2,)),
            pltpu.SemaphoreType.DMA((2 * NT, NCH)),
            pltpu.SemaphoreType.DMA((2 * NT, len(STEPS))),
            pltpu.SemaphoreType.DMA((2 * NT, 2)),
            pltpu.SemaphoreType.DMA((2 * NT, 2)),
        ],
        compiler_params=pltpu.CompilerParams(collective_id=0, has_side_effects=True, vmem_limit_bytes=52 << 20),
        name="block",
    )(latents.reshape(TOK, C), conv_weight.reshape(3, 3 * C, C), conv_bias, w_query, w_keyval, w_out)
    return result.reshape(latents.shape)


def solution(mesh):
    return jax.shard_map(
        per_device,
        mesh=mesh,
        in_specs=(P("frame", "band", None, None), P(), P(), P(), P(), P()),
        out_specs=P("frame", "band", None, None),
        check_vma=False,
    )
```
